32 devices in a mesh: section: 2 (over core), row: 4 (over y, x), col: 4 (over z).
Axes of the slice: x: 2, y: 2, z: 4, core: 2. Of those that a mesh axis runs over, the one named last changes fastest.
Arguments:
- tables: bfloat16 [32, 1024, 256], P('col', ('section', 'row')), may hold values from -1.5 to 1.5
- bag_index: int32 [128, 32, 32], P(None, 'col'), may hold values from 0 to 1024, as said below
- cross_weight: bfloat16 [2, 8192, 8192], P(None, 'col', ('section', 'row')), may hold values from -0.0625 to 0.0625
- cross_bias: float32 [2, 8192], replicated, may hold values from -3 to 3
- upstream: bfloat16 [128, 8192], P(('section', 'row'), 'col'), may hold values from -6 to 6
Outputs:
- crossed: bfloat16 [128, 8192], P(('section', 'row'), 'col')
- pooled_grad: float32 [128, 8192], P(('section', 'row'), 'col')
- table_grad: float32 [32, 1024, 256], P('col', ('section', 'row'))
- weight_grad: float32 [2, 8192, 8192], P(None, 'col', ('section', 'row'))
- bias_grad: float32 [2, 8192], P(None, ('section', 'row'))
The draws below stay inside these ranges and needn't reach their ends.
Inputs may be any that keep to these rules, and one draw needn't show every extreme that they name: `bag_index`: each bag lists 1 to 32 table rows first, then only the padding value 1024, which stands for a zero row.
All inputs are finite; a program needn't handle non-finite values.
Results may differ from the reference program's by a relative error of at most 0.012.
Values may be sent and summed in bfloat16 or wider, within the bound.
A program may use at most 128 MiB of HBM per device.

```python
import jax
import jax.numpy as jnp
from jax import lax

F = 32
E = 256
BAG = 32
LAYERS = 2
D = 8192
BATCH = 128
VOCAB = 1024


def draw_bag_index(key, part):
    base_key = jax.random.fold_in(key, 11)
    length_key, row_key = jax.random.split(base_key)
    lengths = jax.random.randint(length_key, (BATCH, F, 1), 1, BAG + 1)
    row_ids = jax.random.randint(row_key, (BATCH, F, BAG), 0, VOCAB)
    positions = lax.broadcasted_iota(jnp.int32, (BATCH, F, BAG), 2)
    return jnp.where(positions < lengths, row_ids, VOCAB).astype(jnp.int32)


def steps_of(stream_key, extent, cuts, least, high):
    def one(axis_at, parts):
        heights = jax.random.uniform(jax.random.fold_in(jax.random.fold_in(stream_key, 6), axis_at), (parts,), jnp.float32, least / len(cuts), high / len(cuts))
        return jnp.repeat(jnp.exp(heights), extent[axis_at] // parts).reshape((-1,) + (1,) * (len(extent) - axis_at - 1))

    loudness = one(*cuts[0])
    for cut in cuts[1:]:
        loudness = loudness * one(*cut)
    return loudness


def normal_values(stream_key, shape, width, reach, pieces=(), kind=jnp.bfloat16):
    drawn = width * jax.random.normal(stream_key, shape, jnp.float32)
    if pieces:
        drawn = drawn * steps_of(stream_key, shape, pieces, -0.22, 0.18)
    return jnp.clip(drawn, -reach, reach).astype(kind)


def setup_inputs(seed: int = 0) -> dict:
    key_of = jax.random.split(jax.random.key(seed), 6)
    tables = normal_values(key_of[0], (F, VOCAB, E), 0.25, 1.5, ((0, 4), (1, 8)))
    bag_index = draw_bag_index(jax.random.fold_in(key_of[5], 71), 0)
    cross_weight = normal_values(key_of[2], (LAYERS, D, D), D ** -0.5, 0.0625, ((1, 4), (2, 8)))
    cross_bias = normal_values(key_of[3], (LAYERS, D), 0.5, 3.0, (), jnp.float32)
    upstream = normal_values(key_of[4], (BATCH, D), 1.0, 6.0, ((0, 8), (1, 4)))
    return {"tables": tables, "bag_index": bag_index, "cross_weight": cross_weight, "cross_bias": cross_bias, "upstream": upstream}


def pool_feature(operands):
    table_rows, bag_rows = operands
    padded = jnp.concatenate([table_rows, jnp.zeros((1, table_rows.shape[1]), table_rows.dtype)], axis=0)
    picked = jnp.take(padded, bag_rows, axis=0)
    return jnp.sum(picked.astype(jnp.float32), axis=1)


def spread_feature(operands):
    bag_rows, grad_rows = operands
    values = jnp.broadcast_to(grad_rows[:, None, :], (BATCH, BAG, E)).reshape(BATCH * BAG, E)
    summed = jax.ops.segment_sum(values, bag_rows.reshape(-1), num_segments=VOCAB + 1)
    return summed[:VOCAB]


def reference(tables, bag_index, cross_weight, cross_bias, upstream):
    index_major = jnp.transpose(bag_index, (1, 0, 2))
    pooled_parts = lax.map(pool_feature, (tables, index_major))
    pooled = jnp.transpose(pooled_parts, (1, 0, 2)).reshape(BATCH, D).astype(jnp.bfloat16)
    pooled_wide = pooled.astype(jnp.float32)
    current = pooled
    inputs = []
    outputs = []
    for layer_at in range(LAYERS):
        mixed_out = jnp.dot(current, cross_weight[layer_at], preferred_element_type=jnp.float32) + cross_bias[layer_at]
        inputs.append(current)
        outputs.append(mixed_out)
        current = (pooled_wide * mixed_out + current.astype(jnp.float32)).astype(jnp.bfloat16)
    crossed = current
    gradient = upstream.astype(jnp.float32)
    carried = jnp.zeros((BATCH, D), jnp.float32)
    weight_grads = [None] * LAYERS
    bias_grads = [None] * LAYERS
    for layer_at in reversed(range(LAYERS)):
        delta_rows = (pooled_wide * gradient).astype(jnp.bfloat16)
        weight_grads[layer_at] = jnp.dot(inputs[layer_at].T, delta_rows, preferred_element_type=jnp.float32)
        bias_grads[layer_at] = jnp.sum(delta_rows.astype(jnp.float32), axis=0)
        carried = carried + gradient * outputs[layer_at]
        gradient = gradient + jnp.dot(delta_rows, cross_weight[layer_at].T, preferred_element_type=jnp.float32)
    pooled_grad = gradient + carried
    rounded = lax.optimization_barrier(pooled_grad.astype(jnp.bfloat16)).astype(jnp.float32)
    per_feature = jnp.transpose(rounded.reshape(BATCH, F, E), (1, 0, 2))
    table_grad = lax.map(spread_feature, (index_major, per_feature))
    return crossed, pooled_grad, table_grad, jnp.stack(weight_grads), jnp.stack(bias_grads)
```

```python
import functools
import math

import jax
import jax.numpy as jnp
from jax import lax
from jax.experimental import pallas as pl
from jax.experimental.pallas import tpu as pltpu
from jax.sharding import PartitionSpec as P

MESH = pl.DeviceIdType.MESH


def bag_counts(local_ids, shard_rows):
    slot_ids = lax.broadcasted_iota(jnp.int32, (1, 1, shard_rows), 2)
    bag_len = local_ids.shape[1]
    group_size = math.gcd(bag_len, 8)
    summed = jnp.zeros((local_ids.shape[0], shard_rows), jnp.float32)
    for offset in range(0, bag_len, group_size):
        matches = local_ids[:, offset : offset + group_size, None] == slot_ids
        summed = summed + jnp.sum(matches, axis=1, dtype=jnp.float32)
    return summed.astype(jnp.bfloat16)


def tile_of(width):
    return math.gcd(width, 256)


def kernel(
    sizes,
    counts,
    tables,
    up,
    bias,
    w_hbm,
    xa_out,
    db_out,
    crossed_out,
    pgrad_out,
    ga_out,
    w,
    part,
    pr,
    xa,
    db,
    ga,
    drow,
    mpart,
    mr,
    gpart,
    gr,
    mixed,
    w_sem,
    rs_send,
    rs_recv,
    ag_send,
    ag_recv,
    b_send,
    b_recv,
    m_send,
    m_recv,
    g_send,
    g_recv,
):
    section_count, row_count, C = sizes
    N = section_count * row_count
    L, IW, OW = w.shape
    B = xa.shape[1]
    R = B // N
    r = IW // OW
    feats, _, entry = tables.shape
    n = lax.axis_index("section") * row_count + lax.axis_index("row")
    c = lax.axis_index("col")
    home = n // r
    half = n % r

    def device(np_at, col_at):
        return (np_at // row_count, np_at % row_count, col_at)

    def rows_of(np_at):
        return pl.ds(pl.multiple_of(np_at * R, R), R)

    my_rows = rows_of(n)

    barrier = pltpu.get_barrier_semaphore()
    total = N * C
    me = n * C + c

    @pl.loop(1, total)
    def _(d):
        other = lax.rem(me + d, total)
        pl.semaphore_signal(
            barrier, inc=1, device_id=device(other // C, other % C), device_id_type=MESH
        )

    loads = []
    for layer in range(L):
        load = pltpu.make_async_copy(w_hbm.at[layer], w.at[layer], w_sem.at[layer])
        load.start()
        loads.append(load)

    for f in range(feats):
        part[:, f * entry : (f + 1) * entry] = jnp.dot(
            counts[f], tables[f], preferred_element_type=jnp.float32
        ).astype(jnp.bfloat16)

    pl.semaphore_wait(barrier, total - 1)

    sent = []

    def scatter_plane(src, dst, send_sem, recv_sem):
        copies = []
        for d in range(1, N):
            to = lax.rem(n + d, N)
            copy = pltpu.make_async_remote_copy(
                src_ref=src.at[rows_of(to)],
                dst_ref=dst.at[d],
                send_sem=send_sem.at[d],
                recv_sem=recv_sem.at[d],
                device_id=device(to, c),
                device_id_type=MESH,
            )
            copy.start()
            copies.append(copy)
        sent.extend(copies)
        return copies

    def sum_plane(copies, src, dst):
        value = src[my_rows, :].astype(jnp.float32)
        for d in range(1, N):
            copies[d - 1].wait_recv()
            value = value + dst[d].astype(jnp.float32)
        return value

    def gather_plane(buf, send_sem, recv_sem):
        copies = []
        for d in range(1, N):
            to = lax.rem(n + d, N)
            copy = pltpu.make_async_remote_copy(
                src_ref=buf.at[my_rows],
                dst_ref=buf.at[my_rows],
                send_sem=send_sem.at[d],
                recv_sem=recv_sem.at[d],
                device_id=device(to, c),
                device_id_type=MESH,
            )
            copy.start()
            copies.append(copy)
        sent.extend(copies)
        return copies

    def wait_plane(copies):
        for copy in copies:
            copy.wait_recv()

    finals = []

    def send_to_features(rows, buf, send_sem, recv_sem):
        for h in range(r):
            for dc in range(C):
                src = rows.at[:, h * OW : (h + 1) * OW]
                to_np = c * r + h
                to_c = lax.rem(c + dc, C)
                copy = pltpu.make_async_remote_copy(
                    src_ref=src,
                    dst_ref=buf.at[my_rows],
                    send_sem=send_sem.at[h * C + dc],
                    recv_sem=recv_sem.at[n],
                    device_id=device(to_np, to_c),
                    device_id_type=MESH,
                )
                if dc == 0:
                    mine = to_np == n

                    @pl.when(mine)
                    def _():
                        pltpu.make_async_copy(src, buf.at[my_rows], recv_sem.at[n]).start()

                    @pl.when(jnp.logical_not(mine))
                    def _():
                        copy.start()

                    finals.append((jnp.logical_not(mine), copy))
                else:
                    copy.start()
                    sent.append(copy)

    def wait_features(buf, recv_sem):
        for s in range(N):
            piece = buf.at[s * R : (s + 1) * R]
            pltpu.make_async_copy(piece, piece, recv_sem.at[s]).wait()

    def send_to_rows(src, dst, send_sem, recv_sem):
        slot = half * C + c
        for dn in range(N):
            to = lax.rem(n + dn, N)
            copy = pltpu.make_async_remote_copy(
                src_ref=src.at[rows_of(to)],
                dst_ref=dst.at[slot],
                send_sem=send_sem.at[dn],
                recv_sem=recv_sem.at[slot],
                device_id=device(to, home),
                device_id_type=MESH,
            )
            if dn == 0:
                mine = c == home

                @pl.when(mine)
                def _():
                    pltpu.make_async_copy(
                        src.at[my_rows], dst.at[slot], recv_sem.at[slot]
                    ).start()

                @pl.when(jnp.logical_not(mine))
                def _():
                    copy.start()

                finals.append((jnp.logical_not(mine), copy))
            else:
                copy.start()
                sent.append(copy)

    def wait_rows(dst, recv_sem):
        for slot in range(r * C):
            piece = dst.at[slot]
            pltpu.make_async_copy(piece, piece, recv_sem.at[slot]).wait()

    first = scatter_plane(part, pr, rs_send, rs_recv)
    pooled = sum_plane(first, part, pr).astype(jnp.bfloat16)
    xa[0, my_rows, :] = pooled
    gathers = gather_plane(xa.at[0], ag_send.at[0], ag_recv.at[0])
    pooled_wide = pooled.astype(jnp.float32)
    gradient = up[...].astype(jnp.float32)
    drow[L - 1] = (pooled_wide * gradient).astype(jnp.bfloat16)
    send_to_features(drow.at[L - 1], db.at[L - 1], b_send.at[L - 1], b_recv.at[L - 1])
    current = pooled
    carried = jnp.zeros(gradient.shape, jnp.float32)
    for load in loads:
        load.wait()
    kept = [None] * (L + 1)
    kept[L] = gradient
    for step in range(L):
        back = L - 1 - step
        wait_plane(gathers)
        tile = tile_of(OW)

        @pl.loop(0, OW // tile)
        def _(at):
            cols = pl.ds(pl.multiple_of(at * tile, tile), tile)
            mpart[step, :, cols] = jnp.dot(
                xa[step], w[step, :, cols], preferred_element_type=jnp.float32
            ).astype(jnp.bfloat16)

        send_to_rows(mpart.at[step], mr.at[step], m_send.at[step], m_recv.at[step])
        wait_features(db.at[back], b_recv.at[back])
        wide = tile_of(IW)

        @pl.loop(0, IW // wide)
        def _(at):
            cols = pl.ds(pl.multiple_of(at * wide, wide), wide)
            gpart[back, :, cols] = lax.dot_general(
                db[back],
                w[back, cols, :],
                (((1,), (1,)), ((), ())),
                preferred_element_type=jnp.float32,
            ).astype(jnp.bfloat16)

        sums = scatter_plane(gpart.at[back], gr.at[back], g_send.at[back], g_recv.at[back])
        xa_out[step] = xa[step]
        db_out[back] = db[back]
        wait_rows(mr.at[step], m_recv.at[step])
        for h in range(r):
            value = mr[step, h * C].astype(jnp.float32)
            for col_at in range(1, C):
                value = value + mr[step, h * C + col_at].astype(jnp.float32)
            mixed[step, :, h * OW : (h + 1) * OW] = value
        mixed[step] = mixed[step] + bias[step : step + 1, :]
        current = (pooled_wide * mixed[step] + current.astype(jnp.float32)).astype(jnp.bfloat16)
        if step + 1 < L:
            xa[step + 1, my_rows, :] = current
            gathers = gather_plane(xa.at[step + 1], ag_send.at[step + 1], ag_recv.at[step + 1])
        else:
            crossed_out[...] = current
        kept[back] = kept[back + 1] + sum_plane(sums, gpart.at[back], gr.at[back])
        if back > 0:
            drow[back - 1] = (pooled_wide * kept[back]).astype(jnp.bfloat16)
            send_to_features(
                drow.at[back - 1], db.at[back - 1], b_send.at[back - 1], b_recv.at[back - 1]
            )
    pooled_grad = kept[0]
    for layer in range(L):
        carried = carried + kept[layer + 1] * mixed[layer]
    pooled_grad = kept[0] + carried
    pgrad_out[...] = pooled_grad
    ga[my_rows, :] = pooled_grad.astype(jnp.bfloat16)
    gathers = gather_plane(ga, ag_send.at[L], ag_recv.at[L])
    for copy in sent[: -(N - 1)]:
        copy.wait_send()
    for remote, copy in finals:

        @pl.when(remote)
        def _(copy=copy):
            copy.wait_send()

    wait_plane(gathers)
    ga_out[...] = ga[...]
    for copy in sent[-(N - 1) :]:
        copy.wait_send()


def body(tables, bag_index, cross_weight, cross_bias, upstream):
    feat_count, shard_rows, entry_width = tables.shape
    batch_rows = bag_index.shape[0]
    layers, in_width, out_width = cross_weight.shape
    block_rows = upstream.shape[0]
    sizes = tuple(lax.axis_size(axis) for axis in ("section", "row", "col"))
    np_count = sizes[0] * sizes[1]
    col_count = sizes[2]
    ratio = in_width // out_width
    my_row = lax.axis_index(("section", "row"))
    local_ids = bag_index - my_row * shard_rows
    counts = jnp.stack(
        [bag_counts(local_ids[:, feature_at, :], shard_rows) for feature_at in range(feat_count)]
    )
    bias = lax.dynamic_slice_in_dim(cross_bias, lax.axis_index("col") * in_width, in_width, axis=1)
    bf16, f32 = jnp.bfloat16, jnp.float32
    vmem = pl.BlockSpec(memory_space=pltpu.VMEM)
    dma = pltpu.SemaphoreType.DMA
    xa, db, crossed, pooled_grad, full_grad = pl.pallas_call(
        functools.partial(kernel, sizes),
        out_shape=(
            jax.ShapeDtypeStruct((layers, batch_rows, in_width), bf16),
            jax.ShapeDtypeStruct((layers, batch_rows, out_width), bf16),
            jax.ShapeDtypeStruct((block_rows, in_width), bf16),
            jax.ShapeDtypeStruct((block_rows, in_width), f32),
            jax.ShapeDtypeStruct((batch_rows, in_width), bf16),
        ),
        in_specs=[vmem, vmem, vmem, vmem, pl.BlockSpec(memory_space=pl.ANY)],
        out_specs=(vmem,) * 5,
        scratch_shapes=[
            pltpu.VMEM((layers, in_width, out_width), bf16),
            pltpu.VMEM((batch_rows, in_width), bf16),
            pltpu.VMEM((np_count, block_rows, in_width), bf16),
            pltpu.VMEM((layers, batch_rows, in_width), bf16),
            pltpu.VMEM((layers, batch_rows, out_width), bf16),
            pltpu.VMEM((batch_rows, in_width), bf16),
            pltpu.VMEM((layers, block_rows, in_width), bf16),
            pltpu.VMEM((layers, batch_rows, out_width), bf16),
            pltpu.VMEM((layers, ratio * col_count, block_rows, out_width), bf16),
            pltpu.VMEM((layers, batch_rows, in_width), bf16),
            pltpu.VMEM((layers, np_count, block_rows, in_width), bf16),
            pltpu.VMEM((layers, block_rows, in_width), f32),
            dma((layers,)),
            dma((np_count,)),
            dma((np_count,)),
            dma((layers + 1, np_count)),
            dma((layers + 1, np_count)),
            dma((layers, ratio * col_count)),
            dma((layers, np_count)),
            dma((layers, np_count)),
            dma((layers, ratio * col_count)),
            dma((layers, np_count)),
            dma((layers, np_count)),
        ],
        compiler_params=pltpu.CompilerParams(
            collective_id=0, has_side_effects=True, vmem_limit_bytes=56 * 1024 * 1024
        ),
    )(counts, tables, upstream, bias, cross_weight)
    weight_grad = jnp.einsum("lbi,lbo->lio", xa, db, preferred_element_type=f32)
    bias_grad = jnp.sum(db, axis=1, dtype=f32)
    grad_rows_full = full_grad.reshape(batch_rows, feat_count, entry_width)
    table_grad = jnp.einsum("fbv,bfe->fve", counts, grad_rows_full, preferred_element_type=f32)
    return crossed, pooled_grad, table_grad, weight_grad, bias_grad


def solution(mesh):
    return jax.shard_map(
        body,
        mesh=mesh,
        in_specs=(
            P("col", ("section", "row"), None),
            P(None, "col", None),
            P(None, "col", ("section", "row")),
            P(),
            P(("section", "row"), "col"),
        ),
        out_specs=(
            P(("section", "row"), "col"),
            P(("section", "row"), "col"),
            P("col", ("section", "row"), None),
            P(None, "col", ("section", "row")),
            P(None, ("section", "row")),
        ),
        check_vma=False,
    )
```

```python
import functools
import math

import jax
import jax.numpy as jnp
from jax import lax
from jax.experimental import pallas as pl
from jax.experimental.pallas import tpu as pltpu
from jax.sharding import PartitionSpec as P

MESH = pl.DeviceIdType.MESH


def tile_of(width):
    return math.gcd(width, 256)


def kernel(
    sizes,
    ids,
    tables,
    up,
    bias,
    w_hbm,
    counts_out,
    xa_out,
    db_out,
    crossed_out,
    pgrad_out,
    ga_out,
    w,
    part,
    pr,
    pair,
    xa,
    db,
    ga,
    drow,
    mpart,
    mr,
    gpart,
    gr,
    mixed,
    w_sem,
    rs_send,
    rs_recv,
    ag_send,
    ag_recv,
    b_send,
    b_recv,
    m_send,
    m_recv,
    g_send,
    g_recv,
):
    section_count, row_count, C = sizes
    N = section_count * row_count
    L, IW, OW = w.shape
    B = xa.shape[1]
    R = B // N
    r = IW // OW
    feats, shard_rows, entry = tables.shape
    bag_len = ids.shape[1]
    my_section = lax.axis_index("section")
    my_row = lax.axis_index("row")
    n = lax.axis_index("section") * row_count + lax.axis_index("row")
    c = lax.axis_index("col")
    home = n // r
    half = n % r

    def device(np_at, col_at):
        return (np_at // row_count, np_at % row_count, col_at)

    def rows_of(np_at):
        return pl.ds(pl.multiple_of(np_at * R, R), R)

    my_rows = rows_of(n)

    barrier = pltpu.get_barrier_semaphore()
    total = N * C
    me = n * C + c

    @pl.loop(1, total)
    def _(d):
        other = lax.rem(me + d, total)
        pl.semaphore_signal(
            barrier, inc=1, device_id=device(other // C, other % C), device_id_type=MESH
        )

    loads = []
    for layer in range(L):
        load = pltpu.make_async_copy(w_hbm.at[layer], w.at[layer], w_sem.at[layer])
        load.start()
        loads.append(load)

    slots = lax.broadcasted_iota(jnp.int32, (shard_rows, B), 0) + n * shard_rows

    @pl.loop(0, feats)
    def _(f):
        hits = jnp.zeros((shard_rows, B), jnp.int32)
        for j in range(bag_len):
            hits = hits + jnp.where(ids[f, j : j + 1, :] == slots, 1, 0)
        counts = hits.astype(jnp.float32).astype(jnp.bfloat16)
        counts_out[f] = counts
        cols = pl.ds(pl.multiple_of(f * entry, entry), entry)
        part[:, cols] = lax.dot_general(
            counts, tables[f], (((0,), (0,)), ((), ())), preferred_element_type=jnp.float32
        ).astype(jnp.bfloat16)

    pl.semaphore_wait(barrier, total - 1)

    sent = []

    def remote(src, dst, send_sem, recv_sem, section, row):
        copy = pltpu.make_async_remote_copy(
            src_ref=src,
            dst_ref=dst,
            send_sem=send_sem,
            recv_sem=recv_sem,
            device_id=(section, row, c),
            device_id_type=MESH,
        )
        copy.start()
        sent.append(copy)
        return copy

    row_order = list(range(1, row_count)) + [0]

    def scatter_plane(src, dst, pairs, send_sem, recv_sem):
        twins = {}
        for dr in row_order:
            row = lax.rem(my_row + dr, row_count)
            for ds in range(1, section_count):
                at = ds * row_count + dr
                section = lax.rem(my_section + ds, section_count)
                twins[at] = remote(
                    src.at[rows_of(section * row_count + row)],
                    dst.at[at],
                    send_sem.at[at],
                    recv_sem.at[at],
                    section,
                    my_row,
                )
        return src, dst, pairs, send_sem, recv_sem, twins

    def with_twins(scatter, dr):
        src, dst, _, _, _, twins = scatter
        row = lax.rem(my_row + dr, row_count)
        value = src[rows_of(my_section * row_count + row), :].astype(jnp.float32)
        for ds in range(1, section_count):
            at = ds * row_count + dr
            twins[at].wait_recv()
            value = value + dst[at].astype(jnp.float32)
        return value

    def relay_plane(scatter):
        _, dst, pairs, send_sem, recv_sem, _ = scatter
        across = []
        for dr in range(1, row_count):
            pairs[dr] = with_twins(scatter, dr).astype(jnp.bfloat16)
            row = lax.rem(my_row + dr, row_count)
            across.append(
                remote(
                    pairs.at[dr], dst.at[dr], send_sem.at[dr], recv_sem.at[dr], my_section, row
                )
            )
        return scatter, across

    def sum_plane(relayed):
        scatter, across = relayed
        value = with_twins(scatter, 0)
        for dr in range(1, row_count):
            across[dr - 1].wait_recv()
            value = value + scatter[1][dr].astype(jnp.float32)
        return value

    def gather_plane(buf, send_sem, recv_sem):
        across = []
        mine = buf.at[my_rows]
        for dr in range(1, row_count):
            row = lax.rem(my_row + dr, row_count)
            across.append(
                remote(mine, mine, send_sem.at[dr], recv_sem.at[dr], my_section, row)
            )
        waits = []
        for ds in range(1, section_count):
            at = ds * row_count
            section = lax.rem(my_section + ds, section_count)
            waits.append(remote(mine, mine, send_sem.at[at], recv_sem.at[at], section, my_row))
        return buf, send_sem, recv_sem, across, waits

    def wait_plane(gather):
        buf, send_sem, recv_sem, across, waits = gather
        for dr in range(1, row_count):
            across[dr - 1].wait_recv()
            row = lax.rem(my_row + row_count - dr, row_count)
            piece = buf.at[rows_of(my_section * row_count + row)]
            for ds in range(1, section_count):
                at = ds * row_count + dr
                section = lax.rem(my_section + ds, section_count)
                waits.append(
                    remote(piece, piece, send_sem.at[at], recv_sem.at[at], section, my_row)
                )
        for copy in waits:
            copy.wait_recv()

    finals = []

    def send_to_features(rows, buf, send_sem, recv_sem):
        for h in range(r):
            for dc in range(C):
                src = rows.at[:, h * OW : (h + 1) * OW]
                to_np = c * r + h
                to_c = lax.rem(c + dc, C)
                copy = pltpu.make_async_remote_copy(
                    src_ref=src,
                    dst_ref=buf.at[my_rows],
                    send_sem=send_sem.at[h * C + dc],
                    recv_sem=recv_sem.at[n],
                    device_id=device(to_np, to_c),
                    device_id_type=MESH,
                )
                if dc == 0:
                    mine = to_np == n

                    @pl.when(mine)
                    def _():
                        pltpu.make_async_copy(src, buf.at[my_rows], recv_sem.at[n]).start()

                    @pl.when(jnp.logical_not(mine))
                    def _():
                        copy.start()

                    finals.append((jnp.logical_not(mine), copy))
                else:
                    copy.start()
                    sent.append(copy)

    def wait_features(buf, recv_sem):
        for s in range(N):
            piece = buf.at[s * R : (s + 1) * R]
            pltpu.make_async_copy(piece, piece, recv_sem.at[s]).wait()

    def send_to_rows(src, dst, send_sem, recv_sem):
        slot = half * C + c
        for dn in range(N):
            to = lax.rem(n + dn, N)
            copy = pltpu.make_async_remote_copy(
                src_ref=src.at[rows_of(to)],
                dst_ref=dst.at[slot],
                send_sem=send_sem.at[dn],
                recv_sem=recv_sem.at[slot],
                device_id=device(to, home),
                device_id_type=MESH,
            )
            if dn == 0:
                mine = c == home

                @pl.when(mine)
                def _():
                    pltpu.make_async_copy(
                        src.at[my_rows], dst.at[slot], recv_sem.at[slot]
                    ).start()

                @pl.when(jnp.logical_not(mine))
                def _():
                    copy.start()

                finals.append((jnp.logical_not(mine), copy))
            else:
                copy.start()
                sent.append(copy)

    def wait_rows(dst, recv_sem):
        for slot in range(r * C):
            piece = dst.at[slot]
            pltpu.make_async_copy(piece, piece, recv_sem.at[slot]).wait()

    first = relay_plane(scatter_plane(part, pr, pair.at[L], rs_send, rs_recv))
    pooled = sum_plane(first).astype(jnp.bfloat16)
    xa[0, my_rows, :] = pooled
    gathers = gather_plane(xa.at[0], ag_send.at[0], ag_recv.at[0])
    pooled_wide = pooled.astype(jnp.float32)
    gradient = up[...].astype(jnp.float32)
    drow[L - 1] = (pooled_wide * gradient).astype(jnp.bfloat16)
    send_to_features(drow.at[L - 1], db.at[L - 1], b_send.at[L - 1], b_recv.at[L - 1])
    current = pooled
    carried = jnp.zeros(gradient.shape, jnp.float32)
    for load in loads:
        load.wait()
    kept = [None] * (L + 1)
    kept[L] = gradient
    for step in range(L):
        back = L - 1 - step
        wait_plane(gathers)
        tile = tile_of(OW)

        @pl.loop(0, OW // tile)
        def _(at):
            cols = pl.ds(pl.multiple_of(at * tile, tile), tile)
            mpart[step, :, cols] = jnp.dot(
                xa[step], w[step, :, cols], preferred_element_type=jnp.float32
            ).astype(jnp.bfloat16)

        send_to_rows(mpart.at[step], mr.at[step], m_send.at[step], m_recv.at[step])
        wait_features(db.at[back], b_recv.at[back])
        wide = tile_of(IW)

        @pl.loop(0, IW // wide)
        def _(at):
            cols = pl.ds(pl.multiple_of(at * wide, wide), wide)
            gpart[back, :, cols] = lax.dot_general(
                db[back],
                w[back, cols, :],
                (((1,), (1,)), ((), ())),
                preferred_element_type=jnp.float32,
            ).astype(jnp.bfloat16)

        sums = scatter_plane(
            gpart.at[back], gr.at[back], pair.at[back], g_send.at[back], g_recv.at[back]
        )
        xa_out[step] = xa[step]
        db_out[back] = db[back]
        sums = relay_plane(sums)
        wait_rows(mr.at[step], m_recv.at[step])
        for h in range(r):
            value = mr[step, h * C].astype(jnp.float32)
            for col_at in range(1, C):
                value = value + mr[step, h * C + col_at].astype(jnp.float32)
            mixed[step, :, h * OW : (h + 1) * OW] = value
        mixed[step] = mixed[step] + bias[step : step + 1, pl.ds(pl.multiple_of(c * IW, IW), IW)]
        current = (pooled_wide * mixed[step] + current.astype(jnp.float32)).astype(jnp.bfloat16)
        if step + 1 < L:
            xa[step + 1, my_rows, :] = current
            gathers = gather_plane(xa.at[step + 1], ag_send.at[step + 1], ag_recv.at[step + 1])
        else:
            crossed_out[...] = current
        kept[back] = kept[back + 1] + sum_plane(sums)
        if back > 0:
            drow[back - 1] = (pooled_wide * kept[back]).astype(jnp.bfloat16)
            send_to_features(
                drow.at[back - 1], db.at[back - 1], b_send.at[back - 1], b_recv.at[back - 1]
            )
    pooled_grad = kept[0]
    for layer in range(L):
        carried = carried + kept[layer + 1] * mixed[layer]
    pooled_grad = kept[0] + carried
    pgrad_out[...] = pooled_grad
    ga[my_rows, :] = pooled_grad.astype(jnp.bfloat16)
    gathers = gather_plane(ga, ag_send.at[L], ag_recv.at[L])
    wait_plane(gathers)
    ga_out[...] = ga[...]
    for copy in sent:
        copy.wait_send()
    for sent_off, copy in finals:

        @pl.when(sent_off)
        def _(copy=copy):
            copy.wait_send()


def weight_kernel(xa, db, weight_grad, bias_grad):
    weight_grad[0] = lax.dot_general(
        xa[0], db[0], (((0,), (0,)), ((), ())), preferred_element_type=jnp.float32
    )

    @pl.when(pl.program_id(1) == 0)
    def _():
        bias_grad[0] = jnp.sum(db[0].astype(jnp.float32), axis=0, keepdims=True)


def weight_grads(xa, db):
    layers, batch_rows, in_width = xa.shape
    out_width = db.shape[2]
    tile = math.gcd(in_width, 512)
    weight_grad, bias_grad = pl.pallas_call(
        weight_kernel,
        grid=(layers, in_width // tile),
        out_shape=(
            jax.ShapeDtypeStruct((layers, in_width, out_width), jnp.float32),
            jax.ShapeDtypeStruct((layers, 1, out_width), jnp.float32),
        ),
        in_specs=[
            pl.BlockSpec((1, batch_rows, tile), lambda l, i: (l, 0, i)),
            pl.BlockSpec((1, batch_rows, out_width), lambda l, i: (l, 0, 0)),
        ],
        out_specs=(
            pl.BlockSpec((1, tile, out_width), lambda l, i: (l, i, 0)),
            pl.BlockSpec((1, 1, out_width), lambda l, i: (l, 0, 0)),
        ),
    )(xa, db)
    return weight_grad, bias_grad.reshape(layers, out_width)


def body(tables, bag_index, cross_weight, cross_bias, upstream):
    feat_count, shard_rows, entry_width = tables.shape
    batch_rows = bag_index.shape[0]
    layers, in_width, out_width = cross_weight.shape
    block_rows = upstream.shape[0]
    sizes = tuple(lax.axis_size(axis) for axis in ("section", "row", "col"))
    np_count = sizes[0] * sizes[1]
    col_count = sizes[2]
    ratio = in_width // out_width
    ids = jnp.transpose(bag_index, (1, 2, 0))
    bf16, f32 = jnp.bfloat16, jnp.float32
    vmem = pl.BlockSpec(memory_space=pltpu.VMEM)
    dma = pltpu.SemaphoreType.DMA
    counts, xa, db, crossed, pooled_grad, full_grad = pl.pallas_call(
        functools.partial(kernel, sizes),
        out_shape=(
            jax.ShapeDtypeStruct((feat_count, shard_rows, batch_rows), bf16),
            jax.ShapeDtypeStruct((layers, batch_rows, in_width), bf16),
            jax.ShapeDtypeStruct((layers, batch_rows, out_width), bf16),
            jax.ShapeDtypeStruct((block_rows, in_width), bf16),
            jax.ShapeDtypeStruct((block_rows, in_width), f32),
            jax.ShapeDtypeStruct((batch_rows, in_width), bf16),
        ),
        in_specs=[vmem, vmem, vmem, vmem, pl.BlockSpec(memory_space=pl.ANY)],
        out_specs=(vmem,) * 6,
        scratch_shapes=[
            pltpu.VMEM((layers, in_width, out_width), bf16),
            pltpu.VMEM((batch_rows, in_width), bf16),
            pltpu.VMEM((np_count, block_rows, in_width), bf16),
            pltpu.VMEM((layers + 1, sizes[1], block_rows, in_width), bf16),
            pltpu.VMEM((layers, batch_rows, in_width), bf16),
            pltpu.VMEM((layers, batch_rows, out_width), bf16),
            pltpu.VMEM((batch_rows, in_width), bf16),
            pltpu.VMEM((layers, block_rows, in_width), bf16),
            pltpu.VMEM((layers, batch_rows, out_width), bf16),
            pltpu.VMEM((layers, ratio * col_count, block_rows, out_width), bf16),
            pltpu.VMEM((layers, batch_rows, in_width), bf16),
            pltpu.VMEM((layers, np_count, block_rows, in_width), bf16),
            pltpu.VMEM((layers, block_rows, in_width), f32),
            dma((layers,)),
            dma((np_count,)),
            dma((np_count,)),
            dma((layers + 1, np_count)),
            dma((layers + 1, np_count)),
            dma((layers, ratio * col_count)),
            dma((layers, np_count)),
            dma((layers, np_count)),
            dma((layers, ratio * col_count)),
            dma((layers, np_count)),
            dma((layers, np_count)),
        ],
        compiler_params=pltpu.CompilerParams(
            collective_id=0, has_side_effects=True, vmem_limit_bytes=56 * 1024 * 1024
        ),
    )(ids, tables, upstream, cross_bias, cross_weight)
    weight_grad, bias_grad = weight_grads(xa, db)
    grad_rows_full = full_grad.reshape(batch_rows, feat_count, entry_width)
    table_grad = jnp.einsum("fvb,bfe->fve", counts, grad_rows_full, preferred_element_type=f32)
    return crossed, pooled_grad, table_grad, weight_grad, bias_grad


def solution(mesh):
    return jax.shard_map(
        body,
        mesh=mesh,
        in_specs=(
            P("col", ("section", "row"), None),
            P(None, "col", None),
            P(None, "col", ("section", "row")),
            P(),
            P(("section", "row"), "col"),
        ),
        out_specs=(
            P(("section", "row"), "col"),
            P(("section", "row"), "col"),
            P("col", ("section", "row"), None),
            P(None, "col", ("section", "row")),
            P(None, ("section", "row")),
        ),
        check_vma=False,
    )
```

```python
import functools
import math

import jax
import jax.numpy as jnp
from jax import lax
from jax.experimental import pallas as pl
from jax.experimental.pallas import tpu as pltpu
from jax.sharding import PartitionSpec as P

MESH = pl.DeviceIdType.MESH


def tile_of(width):
    return math.gcd(width, 256)


def kernel(
    sizes,
    ids,
    tables,
    up,
    bias,
    w_hbm,
    counts_out,
    xa_out,
    db_out,
    crossed_out,
    pgrad_out,
    ga_out,
    w,
    kept_counts,
    part,
    pr,
    pair,
    xa,
    db,
    ga,
    drow,
    mpart,
    mr,
    gpart,
    gr,
    mixed,
    w_sem,
    out_sem,
    rs_send,
    rs_recv,
    ag_send,
    ag_recv,
    b_send,
    b_recv,
    m_send,
    m_recv,
    g_send,
    g_recv,
):
    section_count, row_count, C = sizes
    N = section_count * row_count
    L, IW, OW = w.shape
    B = xa.shape[1]
    R = B // N
    r = IW // OW
    feats, shard_rows, entry = tables.shape
    bag_len = ids.shape[1]
    my_section = lax.axis_index("section")
    my_row = lax.axis_index("row")
    n = lax.axis_index("section") * row_count + lax.axis_index("row")
    c = lax.axis_index("col")
    home = n // r
    half = n % r

    def device(np_at, col_at):
        return (np_at // row_count, np_at % row_count, col_at)

    def rows_of(np_at):
        return pl.ds(pl.multiple_of(np_at * R, R), R)

    my_rows = rows_of(n)

    barrier = pltpu.get_barrier_semaphore()
    total = N * C
    me = n * C + c

    @pl.loop(1, total)
    def _(d):
        other = lax.rem(me + d, total)
        pl.semaphore_signal(
            barrier, inc=1, device_id=device(other // C, other % C), device_id_type=MESH
        )

    loads = []
    for layer in range(L):
        load = pltpu.make_async_copy(w_hbm.at[layer], w.at[layer], w_sem.at[layer])
        load.start()
        loads.append(load)

    slots = lax.broadcasted_iota(jnp.int32, (shard_rows, B), 0) + n * shard_rows

    @pl.loop(0, feats)
    def _(f):
        hits = jnp.zeros((shard_rows, B), jnp.int32)
        for j in range(bag_len):
            hits = hits + jnp.where(ids[f, j : j + 1, :] == slots, 1, 0)
        counts = hits.astype(jnp.float32).astype(jnp.bfloat16)
        kept_counts[f] = counts
        cols = pl.ds(pl.multiple_of(f * entry, entry), entry)
        part[:, cols] = lax.dot_general(
            counts, tables[f], (((0,), (0,)), ((), ())), preferred_element_type=jnp.float32
        ).astype(jnp.bfloat16)

    leaving = []

    def leave(src, dst):
        copy = pltpu.make_async_copy(src, dst, out_sem.at[len(leaving)])
        copy.start()
        leaving.append(copy)

    leave(kept_counts, counts_out)
    pl.semaphore_wait(barrier, total - 1)

    sent = []

    def remote(src, dst, send_sem, recv_sem, section, row):
        copy = pltpu.make_async_remote_copy(
            src_ref=src,
            dst_ref=dst,
            send_sem=send_sem,
            recv_sem=recv_sem,
            device_id=(section, row, c),
            device_id_type=MESH,
        )
        copy.start()
        sent.append(copy)
        return copy

    row_order = list(range(1, row_count)) + [0]

    def scatter_plane(src, dst, pairs, send_sem, recv_sem):
        twins = {}
        for dr in row_order:
            row = lax.rem(my_row + dr, row_count)
            for ds in range(1, section_count):
                at = ds * row_count + dr
                section = lax.rem(my_section + ds, section_count)
                twins[at] = remote(
                    src.at[rows_of(section * row_count + row)],
                    dst.at[at],
                    send_sem.at[at],
                    recv_sem.at[at],
                    section,
                    my_row,
                )
        return src, dst, pairs, send_sem, recv_sem, twins

    def with_twins(scatter, dr):
        src, dst, _, _, _, twins = scatter
        row = lax.rem(my_row + dr, row_count)
        value = src[rows_of(my_section * row_count + row), :].astype(jnp.float32)
        for ds in range(1, section_count):
            at = ds * row_count + dr
            twins[at].wait_recv()
            value = value + dst[at].astype(jnp.float32)
        return value

    def relay_plane(scatter):
        _, dst, pairs, send_sem, recv_sem, _ = scatter
        across = []
        for dr in range(1, row_count):
            pairs[dr] = with_twins(scatter, dr).astype(jnp.bfloat16)
            row = lax.rem(my_row + dr, row_count)
            across.append(
                remote(
                    pairs.at[dr], dst.at[dr], send_sem.at[dr], recv_sem.at[dr], my_section, row
                )
            )
        return scatter, across

    def sum_plane(relayed):
        scatter, across = relayed
        value = with_twins(scatter, 0)
        for dr in range(1, row_count):
            across[dr - 1].wait_recv()
            value = value + scatter[1][dr].astype(jnp.float32)
        return value

    def gather_plane(buf, send_sem, recv_sem):
        across = []
        mine = buf.at[my_rows]
        for dr in range(1, row_count):
            row = lax.rem(my_row + dr, row_count)
            across.append(
                remote(mine, mine, send_sem.at[dr], recv_sem.at[dr], my_section, row)
            )
        waits = []
        for ds in range(1, section_count):
            at = ds * row_count
            section = lax.rem(my_section + ds, section_count)
            waits.append(remote(mine, mine, send_sem.at[at], recv_sem.at[at], section, my_row))
        return buf, send_sem, recv_sem, across, waits

    def wait_plane(gather):
        buf, send_sem, recv_sem, across, waits = gather
        for dr in range(1, row_count):
            across[dr - 1].wait_recv()
            row = lax.rem(my_row + row_count - dr, row_count)
            piece = buf.at[rows_of(my_section * row_count + row)]
            for ds in range(1, section_count):
                at = ds * row_count + dr
                section = lax.rem(my_section + ds, section_count)
                waits.append(
                    remote(piece, piece, send_sem.at[at], recv_sem.at[at], section, my_row)
                )
        for copy in waits:
            copy.wait_recv()

    finals = []

    def send_to_features(rows, buf, send_sem, recv_sem):
        for h in range(r):
            for dc in range(C):
                src = rows.at[:, h * OW : (h + 1) * OW]
                to_np = c * r + h
                to_c = lax.rem(c + dc, C)
                copy = pltpu.make_async_remote_copy(
                    src_ref=src,
                    dst_ref=buf.at[my_rows],
                    send_sem=send_sem.at[h * C + dc],
                    recv_sem=recv_sem.at[n],
                    device_id=device(to_np, to_c),
                    device_id_type=MESH,
                )
                if dc == 0:
                    mine = to_np == n

                    @pl.when(mine)
                    def _():
                        pltpu.make_async_copy(src, buf.at[my_rows], recv_sem.at[n]).start()

                    @pl.when(jnp.logical_not(mine))
                    def _():
                        copy.start()

                    finals.append((jnp.logical_not(mine), copy))
                else:
                    copy.start()
                    sent.append(copy)

    def wait_features(buf, recv_sem):
        for s in range(N):
            piece = buf.at[s * R : (s + 1) * R]
            pltpu.make_async_copy(piece, piece, recv_sem.at[s]).wait()

    def send_to_rows(src, dst, send_sem, recv_sem):
        slot = half * C + c
        for dn in range(N):
            to = lax.rem(n + dn, N)
            copy = pltpu.make_async_remote_copy(
                src_ref=src.at[rows_of(to)],
                dst_ref=dst.at[slot],
                send_sem=send_sem.at[dn],
                recv_sem=recv_sem.at[slot],
                device_id=device(to, home),
                device_id_type=MESH,
            )
            if dn == 0:
                mine = c == home

                @pl.when(mine)
                def _():
                    pltpu.make_async_copy(
                        src.at[my_rows], dst.at[slot], recv_sem.at[slot]
                    ).start()

                @pl.when(jnp.logical_not(mine))
                def _():
                    copy.start()

                finals.append((jnp.logical_not(mine), copy))
            else:
                copy.start()
                sent.append(copy)

    def wait_rows(dst, recv_sem):
        for slot in range(r * C):
            piece = dst.at[slot]
            pltpu.make_async_copy(piece, piece, recv_sem.at[slot]).wait()

    first = relay_plane(scatter_plane(part, pr, pair.at[L], rs_send, rs_recv))
    pooled = sum_plane(first).astype(jnp.bfloat16)
    xa[0, my_rows, :] = pooled
    gathers = gather_plane(xa.at[0], ag_send.at[0], ag_recv.at[0])
    pooled_wide = pooled.astype(jnp.float32)
    gradient = up[...].astype(jnp.float32)
    drow[L - 1] = (pooled_wide * gradient).astype(jnp.bfloat16)
    send_to_features(drow.at[L - 1], db.at[L - 1], b_send.at[L - 1], b_recv.at[L - 1])
    current = pooled
    carried = jnp.zeros(gradient.shape, jnp.float32)
    for load in loads:
        load.wait()
    kept = [None] * (L + 1)
    kept[L] = gradient
    for step in range(L):
        back = L - 1 - step
        wait_plane(gathers)
        tile = tile_of(OW)

        @pl.loop(0, OW // tile)
        def _(at):
            cols = pl.ds(pl.multiple_of(at * tile, tile), tile)
            mpart[step, :, cols] = jnp.dot(
                xa[step], w[step, :, cols], preferred_element_type=jnp.float32
            ).astype(jnp.bfloat16)

        send_to_rows(mpart.at[step], mr.at[step], m_send.at[step], m_recv.at[step])
        wait_features(db.at[back], b_recv.at[back])
        wide = tile_of(IW)

        @pl.loop(0, IW // wide)
        def _(at):
            cols = pl.ds(pl.multiple_of(at * wide, wide), wide)
            gpart[back, :, cols] = lax.dot_general(
                db[back],
                w[back, cols, :],
                (((1,), (1,)), ((), ())),
                preferred_element_type=jnp.float32,
            ).astype(jnp.bfloat16)

        sums = scatter_plane(
            gpart.at[back], gr.at[back], pair.at[back], g_send.at[back], g_recv.at[back]
        )
        leave(xa.at[step], xa_out.at[step])
        leave(db.at[back], db_out.at[back])
        sums = relay_plane(sums)
        wait_rows(mr.at[step], m_recv.at[step])
        for h in range(r):
            value = mr[step, h * C].astype(jnp.float32)
            for col_at in range(1, C):
                value = value + mr[step, h * C + col_at].astype(jnp.float32)
            mixed[step, :, h * OW : (h + 1) * OW] = value
        mixed[step] = mixed[step] + bias[step : step + 1, pl.ds(pl.multiple_of(c * IW, IW), IW)]
        current = (pooled_wide * mixed[step] + current.astype(jnp.float32)).astype(jnp.bfloat16)
        if step + 1 < L:
            xa[step + 1, my_rows, :] = current
            gathers = gather_plane(xa.at[step + 1], ag_send.at[step + 1], ag_recv.at[step + 1])
        else:
            crossed_out[...] = current
        kept[back] = kept[back + 1] + sum_plane(sums)
        if back > 0:
            drow[back - 1] = (pooled_wide * kept[back]).astype(jnp.bfloat16)
            send_to_features(
                drow.at[back - 1], db.at[back - 1], b_send.at[back - 1], b_recv.at[back - 1]
            )
    pooled_grad = kept[0]
    for layer in range(L):
        carried = carried + kept[layer + 1] * mixed[layer]
    pooled_grad = kept[0] + carried
    pgrad_out[...] = pooled_grad
    ga[my_rows, :] = pooled_grad.astype(jnp.bfloat16)
    gathers = gather_plane(ga, ag_send.at[L], ag_recv.at[L])
    wait_plane(gathers)
    leave(ga, ga_out)
    for copy in leaving:
        copy.wait()
    for copy in sent:
        copy.wait_send()
    for sent_off, copy in finals:

        @pl.when(sent_off)
        def _(copy=copy):
            copy.wait_send()


def output_kernel(
    xa_hbm,
    db_hbm,
    counts_hbm,
    ga_hbm,
    crossed_hbm,
    pgrad_hbm,
    weight_grad,
    bias_grad,
    table_grad,
    crossed_out,
    pgrad_out,
    xa,
    db,
    counts,
    ga,
    held,
    load_sem,
    sem,
):
    pairs = (
        (xa_hbm, xa),
        (db_hbm, db),
        (counts_hbm, counts),
        (ga_hbm, ga),
        (crossed_hbm, crossed_out),
        (pgrad_hbm, pgrad_out),
    )
    loads = [
        pltpu.make_async_copy(src, dst, load_sem.at[k]) for k, (src, dst) in enumerate(pairs)
    ]
    for load in loads:
        load.start()
    loads[0].wait()
    loads[1].wait()
    layers, in_width, _ = held.shape
    tile = math.gcd(in_width, 512)
    tiles = in_width // tile
    copies = []
    for layer in range(layers):
        for at in range(tiles):
            rows = slice(at * tile, (at + 1) * tile)
            held[layer, rows, :] = lax.dot_general(
                xa[layer, :, rows],
                db[layer],
                (((0,), (0,)), ((), ())),
                preferred_element_type=jnp.float32,
            )
            copy = pltpu.make_async_copy(
                held.at[layer, rows], weight_grad.at[layer, rows], sem.at[layer * tiles + at]
            )
            copy.start()
            copies.append(copy)
    feats, _, entry = table_grad.shape
    for load in loads[2:]:
        load.wait()
    for f in range(feats):
        table_grad[f] = jnp.dot(
            counts[f], ga[:, f * entry : (f + 1) * entry], preferred_element_type=jnp.float32
        )
    for layer in range(layers):
        bias_grad[layer : layer + 1, :] = jnp.sum(
            db[layer].astype(jnp.float32), axis=0, keepdims=True
        )
    for copy in copies:
        copy.wait()


def write_outputs(xa, db, counts, ga, crossed, pgrad):
    layers, _, in_width = xa.shape
    out_width = db.shape[2]
    feats, shard_rows, _ = counts.shape
    entry = in_width // feats
    tiles = in_width // math.gcd(in_width, 512)
    f32 = jnp.float32
    vmem = pl.BlockSpec(memory_space=pltpu.VMEM)
    return pl.pallas_call(
        output_kernel,
        out_shape=(
            jax.ShapeDtypeStruct((layers, in_width, out_width), f32),
            jax.ShapeDtypeStruct((layers, out_width), f32),
            jax.ShapeDtypeStruct((feats, shard_rows, entry), f32),
            jax.ShapeDtypeStruct(crossed.shape, crossed.dtype),
            jax.ShapeDtypeStruct(pgrad.shape, f32),
        ),
        in_specs=[pl.BlockSpec(memory_space=pl.ANY)] * 6,
        out_specs=(pl.BlockSpec(memory_space=pl.ANY), vmem, vmem, vmem, vmem),
        scratch_shapes=[
            pltpu.VMEM(xa.shape, xa.dtype),
            pltpu.VMEM(db.shape, db.dtype),
            pltpu.VMEM(counts.shape, counts.dtype),
            pltpu.VMEM(ga.shape, ga.dtype),
            pltpu.VMEM((layers, in_width, out_width), f32),
            pltpu.SemaphoreType.DMA((6,)),
            pltpu.SemaphoreType.DMA((layers * tiles,)),
        ],
        compiler_params=pltpu.CompilerParams(vmem_limit_bytes=56 * 1024 * 1024),
    )(xa, db, counts, ga, crossed, pgrad)


def body(tables, bag_index, cross_weight, cross_bias, upstream):
    feat_count, shard_rows, entry_width = tables.shape
    batch_rows = bag_index.shape[0]
    layers, in_width, out_width = cross_weight.shape
    block_rows = upstream.shape[0]
    sizes = tuple(lax.axis_size(axis) for axis in ("section", "row", "col"))
    np_count = sizes[0] * sizes[1]
    col_count = sizes[2]
    ratio = in_width // out_width
    ids = jnp.transpose(bag_index, (1, 2, 0))
    bf16, f32 = jnp.bfloat16, jnp.float32
    vmem = pl.BlockSpec(memory_space=pltpu.VMEM)
    hbm = pl.BlockSpec(memory_space=pl.ANY)
    dma = pltpu.SemaphoreType.DMA
    counts, xa, db, crossed, pooled_grad, full_grad = pl.pallas_call(
        functools.partial(kernel, sizes),
        out_shape=(
            jax.ShapeDtypeStruct((feat_count, shard_rows, batch_rows), bf16),
            jax.ShapeDtypeStruct((layers, batch_rows, in_width), bf16),
            jax.ShapeDtypeStruct((layers, batch_rows, out_width), bf16),
            jax.ShapeDtypeStruct((block_rows, in_width), bf16),
            jax.ShapeDtypeStruct((block_rows, in_width), f32),
            jax.ShapeDtypeStruct((batch_rows, in_width), bf16),
        ),
        in_specs=[vmem, vmem, vmem, vmem, pl.BlockSpec(memory_space=pl.ANY)],
        out_specs=(hbm, hbm, hbm, vmem, vmem, hbm),
        scratch_shapes=[
            pltpu.VMEM((layers, in_width, out_width), bf16),
            pltpu.VMEM((feat_count, shard_rows, batch_rows), bf16),
            pltpu.VMEM((batch_rows, in_width), bf16),
            pltpu.VMEM((np_count, block_rows, in_width), bf16),
            pltpu.VMEM((layers + 1, sizes[1], block_rows, in_width), bf16),
            pltpu.VMEM((layers, batch_rows, in_width), bf16),
            pltpu.VMEM((layers, batch_rows, out_width), bf16),
            pltpu.VMEM((batch_rows, in_width), bf16),
            pltpu.VMEM((layers, block_rows, in_width), bf16),
            pltpu.VMEM((layers, batch_rows, out_width), bf16),
            pltpu.VMEM((layers, ratio * col_count, block_rows, out_width), bf16),
            pltpu.VMEM((layers, batch_rows, in_width), bf16),
            pltpu.VMEM((layers, np_count, block_rows, in_width), bf16),
            pltpu.VMEM((layers, block_rows, in_width), f32),
            dma((layers,)),
            dma((2 * layers + 2,)),
            dma((np_count,)),
            dma((np_count,)),
            dma((layers + 1, np_count)),
            dma((layers + 1, np_count)),
            dma((layers, ratio * col_count)),
            dma((layers, np_count)),
            dma((layers, np_count)),
            dma((layers, ratio * col_count)),
            dma((layers, np_count)),
            dma((layers, np_count)),
        ],
        compiler_params=pltpu.CompilerParams(
            collective_id=0, has_side_effects=True, vmem_limit_bytes=56 * 1024 * 1024
        ),
    )(ids, tables, upstream, cross_bias, cross_weight)
    weight_grad, bias_grad, table_grad, crossed, pooled_grad = write_outputs(
        xa, db, counts, full_grad, crossed, pooled_grad
    )
    return crossed, pooled_grad, table_grad, weight_grad, bias_grad


def solution(mesh):
    return jax.shard_map(
        body,
        mesh=mesh,
        in_specs=(
            P("col", ("section", "row"), None),
            P(None, "col", None),
            P(None, "col", ("section", "row")),
            P(),
            P(("section", "row"), "col"),
        ),
        out_specs=(
            P(("section", "row"), "col"),
            P(("section", "row"), "col"),
            P("col", ("section", "row"), None),
            P(None, "col", ("section", "row")),
            P(None, ("section", "row")),
        ),
        check_vma=False,
    )
```

```python
import functools
import math

import jax
import jax.numpy as jnp
from jax import lax
from jax.experimental import pallas as pl
from jax.experimental.pallas import tpu as pltpu
from jax.sharding import PartitionSpec as P

MESH = pl.DeviceIdType.MESH


def tile_of(width):
    return math.gcd(width, 256)


def kernel(
    sizes,
    ids,
    tables,
    up,
    bias,
    w_hbm,
    counts_out,
    xa_out,
    db_out,
    crossed_out,
    pgrad_out,
    ga_out,
    w,
    kept_counts,
    part,
    pr,
    pair,
    xa,
    db,
    ga,
    drow,
    mpart,
    mr,
    gpart,
    gr,
    mixed,
    w_sem,
    out_sem,
    rs_send,
    rs_recv,
    ag_send,
    ag_recv,
    b_send,
    b_recv,
    m_send,
    m_recv,
    g_send,
    g_recv,
):
    section_count, row_count, C = sizes
    N = section_count * row_count
    L, IW, OW = w.shape
    B = xa.shape[1]
    R = B // N
    r = IW // OW
    feats, shard_rows, entry = tables.shape
    bag_len = ids.shape[1]
    my_section = lax.axis_index("section")
    my_row = lax.axis_index("row")
    n = lax.axis_index("section") * row_count + lax.axis_index("row")
    c = lax.axis_index("col")
    home = n // r
    half = n % r

    def device(np_at, col_at):
        return (np_at // row_count, np_at % row_count, col_at)

    def rows_of(np_at):
        return pl.ds(pl.multiple_of(np_at * R, R), R)

    my_rows = rows_of(n)

    barrier = pltpu.get_barrier_semaphore()
    total = N * C
    me = n * C + c

    @pl.loop(1, total)
    def _(d):
        other = lax.rem(me + d, total)
        pl.semaphore_signal(
            barrier, inc=1, device_id=device(other // C, other % C), device_id_type=MESH
        )

    loads = []
    for layer in range(L):
        load = pltpu.make_async_copy(w_hbm.at[layer], w.at[layer], w_sem.at[layer])
        load.start()
        loads.append(load)

    slots = lax.broadcasted_iota(jnp.int32, (shard_rows, B), 0) + n * shard_rows

    @pl.loop(0, feats)
    def _(f):
        hits = jnp.zeros((shard_rows, B), jnp.int32)
        for j in range(bag_len):
            hits = hits + jnp.where(ids[f, j : j + 1, :] == slots, 1, 0)
        counts = hits.astype(jnp.float32).astype(jnp.bfloat16)
        kept_counts[f] = counts
        cols = pl.ds(pl.multiple_of(f * entry, entry), entry)
        part[:, cols] = lax.dot_general(
            counts, tables[f], (((0,), (0,)), ((), ())), preferred_element_type=jnp.float32
        ).astype(jnp.bfloat16)

    leaving = []

    def leave(src, dst):
        copy = pltpu.make_async_copy(src, dst, out_sem.at[len(leaving)])
        copy.start()
        leaving.append(copy)

    leave(kept_counts, counts_out)
    pl.semaphore_wait(barrier, total - 1)

    sent = []

    def remote(src, dst, send_sem, recv_sem, section, row):
        copy = pltpu.make_async_remote_copy(
            src_ref=src,
            dst_ref=dst,
            send_sem=send_sem,
            recv_sem=recv_sem,
            device_id=(section, row, c),
            device_id_type=MESH,
        )
        copy.start()
        sent.append(copy)
        return copy

    row_order = list(range(1, row_count)) + [0]

    def scatter_plane(src, dst, pairs, send_sem, recv_sem):
        twins = {}
        for dr in row_order:
            row = lax.rem(my_row + dr, row_count)
            for ds in range(1, section_count):
                at = ds * row_count + dr
                section = lax.rem(my_section + ds, section_count)
                twins[at] = remote(
                    src.at[rows_of(section * row_count + row)],
                    dst.at[at],
                    send_sem.at[at],
                    recv_sem.at[at],
                    section,
                    my_row,
                )
        return src, dst, pairs, send_sem, recv_sem, twins

    def with_twins(scatter, dr):
        src, dst, _, _, _, twins = scatter
        row = lax.rem(my_row + dr, row_count)
        value = src[rows_of(my_section * row_count + row), :].astype(jnp.float32)
        for ds in range(1, section_count):
            at = ds * row_count + dr
            twins[at].wait_recv()
            value = value + dst[at].astype(jnp.float32)
        return value

    def relay_plane(scatter):
        _, dst, pairs, send_sem, recv_sem, _ = scatter
        across = []
        for dr in range(1, row_count):
            pairs[dr] = with_twins(scatter, dr).astype(jnp.bfloat16)
            row = lax.rem(my_row + dr, row_count)
            across.append(
                remote(
                    pairs.at[dr], dst.at[dr], send_sem.at[dr], recv_sem.at[dr], my_section, row
                )
            )
        return scatter, across

    def sum_plane(relayed):
        scatter, across = relayed
        value = with_twins(scatter, 0)
        for dr in range(1, row_count):
            across[dr - 1].wait_recv()
            value = value + scatter[1][dr].astype(jnp.float32)
        return value

    def gather_plane(buf, send_sem, recv_sem):
        across = []
        mine = buf.at[my_rows]
        for dr in range(1, row_count):
            row = lax.rem(my_row + dr, row_count)
            across.append(
                remote(mine, mine, send_sem.at[dr], recv_sem.at[dr], my_section, row)
            )
        waits = []
        for ds in range(1, section_count):
            at = ds * row_count
            section = lax.rem(my_section + ds, section_count)
            waits.append(remote(mine, mine, send_sem.at[at], recv_sem.at[at], section, my_row))
        return buf, send_sem, recv_sem, across, waits

    def wait_plane(gather):
        buf, send_sem, recv_sem, across, waits = gather
        for dr in range(1, row_count):
            across[dr - 1].wait_recv()
            row = lax.rem(my_row + row_count - dr, row_count)
            piece = buf.at[rows_of(my_section * row_count + row)]
            for ds in range(1, section_count):
                at = ds * row_count + dr
                section = lax.rem(my_section + ds, section_count)
                waits.append(
                    remote(piece, piece, send_sem.at[at], recv_sem.at[at], section, my_row)
                )
        for copy in waits:
            copy.wait_recv()

    finals = []

    def send_to_features(rows, buf, send_sem, recv_sem):
        for h in range(r):
            for dc in range(C):
                src = rows.at[:, h * OW : (h + 1) * OW]
                to_np = c * r + h
                to_c = lax.rem(c + dc, C)
                copy = pltpu.make_async_remote_copy(
                    src_ref=src,
                    dst_ref=buf.at[my_rows],
                    send_sem=send_sem.at[h * C + dc],
                    recv_sem=recv_sem.at[n],
                    device_id=device(to_np, to_c),
                    device_id_type=MESH,
                )
                if dc == 0:
                    mine = to_np == n

                    @pl.when(mine)
                    def _():
                        pltpu.make_async_copy(src, buf.at[my_rows], recv_sem.at[n]).start()

                    @pl.when(jnp.logical_not(mine))
                    def _():
                        copy.start()

                    finals.append((jnp.logical_not(mine), copy))
                else:
                    copy.start()
                    sent.append(copy)

    def wait_features(buf, recv_sem):
        for s in range(N):
            piece = buf.at[s * R : (s + 1) * R]
            pltpu.make_async_copy(piece, piece, recv_sem.at[s]).wait()

    def send_to_rows(src, dst, send_sem, recv_sem):
        slot = half * C + c
        for dn in range(N):
            to = lax.rem(n + dn, N)
            copy = pltpu.make_async_remote_copy(
                src_ref=src.at[rows_of(to)],
                dst_ref=dst.at[slot],
                send_sem=send_sem.at[dn],
                recv_sem=recv_sem.at[slot],
                device_id=device(to, home),
                device_id_type=MESH,
            )
            if dn == 0:
                mine = c == home

                @pl.when(mine)
                def _():
                    pltpu.make_async_copy(
                        src.at[my_rows], dst.at[slot], recv_sem.at[slot]
                    ).start()

                @pl.when(jnp.logical_not(mine))
                def _():
                    copy.start()

                finals.append((jnp.logical_not(mine), copy))
            else:
                copy.start()
                sent.append(copy)

    def wait_rows(dst, recv_sem):
        for slot in range(r * C):
            piece = dst.at[slot]
            pltpu.make_async_copy(piece, piece, recv_sem.at[slot]).wait()

    first = relay_plane(scatter_plane(part, pr, pair.at[L], rs_send, rs_recv))
    pooled = sum_plane(first).astype(jnp.bfloat16)
    xa[0, my_rows, :] = pooled
    gathers = gather_plane(xa.at[0], ag_send.at[0], ag_recv.at[0])
    pooled_wide = pooled.astype(jnp.float32)
    gradient = up[...].astype(jnp.float32)
    drow[L - 1] = (pooled_wide * gradient).astype(jnp.bfloat16)
    send_to_features(drow.at[L - 1], db.at[L - 1], b_send.at[L - 1], b_recv.at[L - 1])
    current = pooled
    carried = jnp.zeros(gradient.shape, jnp.float32)
    for load in loads:
        load.wait()
    kept = [None] * (L + 1)
    kept[L] = gradient
    for step in range(L):
        back = L - 1 - step
        wait_plane(gathers)
        tile = tile_of(OW)

        @pl.loop(0, OW // tile)
        def _(at):
            cols = pl.ds(pl.multiple_of(at * tile, tile), tile)
            mpart[step, :, cols] = jnp.dot(
                xa[step], w[step, :, cols], preferred_element_type=jnp.float32
            ).astype(jnp.bfloat16)

        send_to_rows(mpart.at[step], mr.at[step], m_send.at[step], m_recv.at[step])
        wait_features(db.at[back], b_recv.at[back])
        wide = tile_of(IW)

        @pl.loop(0, IW // wide)
        def _(at):
            cols = pl.ds(pl.multiple_of(at * wide, wide), wide)
            gpart[back, :, cols] = lax.dot_general(
                db[back],
                w[back, cols, :],
                (((1,), (1,)), ((), ())),
                preferred_element_type=jnp.float32,
            ).astype(jnp.bfloat16)

        sums = scatter_plane(
            gpart.at[back], gr.at[back], pair.at[back], g_send.at[back], g_recv.at[back]
        )
        leave(xa.at[step], xa_out.at[step])
        leave(db.at[back], db_out.at[back])
        sums = relay_plane(sums)
        wait_rows(mr.at[step], m_recv.at[step])
        for h in range(r):
            value = mr[step, h * C].astype(jnp.float32)
            for col_at in range(1, C):
                value = value + mr[step, h * C + col_at].astype(jnp.float32)
            mixed[step, :, h * OW : (h + 1) * OW] = value
        mixed[step] = mixed[step] + bias[step : step + 1, pl.ds(pl.multiple_of(c * IW, IW), IW)]
        current = (pooled_wide * mixed[step] + current.astype(jnp.float32)).astype(jnp.bfloat16)
        if step + 1 < L:
            xa[step + 1, my_rows, :] = current
            gathers = gather_plane(xa.at[step + 1], ag_send.at[step + 1], ag_recv.at[step + 1])
        else:
            crossed_out[...] = current
        kept[back] = kept[back + 1] + sum_plane(sums)
        if back > 0:
            drow[back - 1] = (pooled_wide * kept[back]).astype(jnp.bfloat16)
            send_to_features(
                drow.at[back - 1], db.at[back - 1], b_send.at[back - 1], b_recv.at[back - 1]
            )
    pooled_grad = kept[0]
    for layer in range(L):
        carried = carried + kept[layer + 1] * mixed[layer]
    pooled_grad = kept[0] + carried
    pgrad_out[...] = pooled_grad
    ga[my_rows, :] = pooled_grad.astype(jnp.bfloat16)
    gathers = gather_plane(ga, ag_send.at[L], ag_recv.at[L])
    wait_plane(gathers)
    leave(ga, ga_out)
    for copy in leaving:
        copy.wait()
    for copy in sent:
        copy.wait_send()
    for sent_off, copy in finals:

        @pl.when(sent_off)
        def _(copy=copy):
            copy.wait_send()


def output_kernel(
    xa_hbm,
    db_hbm,
    counts_hbm,
    ga_hbm,
    crossed_hbm,
    pgrad_hbm,
    weight_grad,
    bias_grad,
    table_grad,
    crossed_out,
    pgrad_out,
    xa,
    db,
    counts,
    ga,
    held,
    load_sem,
    sem,
):
    layers, in_width, _ = held.shape
    pairs = (
        *((xa_hbm.at[layer], xa.at[layer]) for layer in range(layers)),
        *((db_hbm.at[layer], db.at[layer]) for layer in range(layers)),
        (counts_hbm, counts),
        (ga_hbm, ga),
        (crossed_hbm, crossed_out),
        (pgrad_hbm, pgrad_out),
    )
    loads = [
        pltpu.make_async_copy(src, dst, load_sem.at[k]) for k, (src, dst) in enumerate(pairs)
    ]
    for load in loads:
        load.start()
    tile = math.gcd(in_width, 256)
    tiles = in_width // tile
    copies = []
    for layer in range(layers):
        loads[layer].wait()
        loads[layers + layer].wait()
        for at in range(tiles):
            rows = slice(at * tile, (at + 1) * tile)
            held[layer, rows, :] = lax.dot_general(
                xa[layer, :, rows],
                db[layer],
                (((0,), (0,)), ((), ())),
                preferred_element_type=jnp.float32,
            )
            copy = pltpu.make_async_copy(
                held.at[layer, rows], weight_grad.at[layer, rows], sem.at[layer * tiles + at]
            )
            copy.start()
            copies.append(copy)
    feats, _, entry = table_grad.shape
    for load in loads[2 * layers :]:
        load.wait()
    for f in range(feats):
        table_grad[f] = jnp.dot(
            counts[f], ga[:, f * entry : (f + 1) * entry], preferred_element_type=jnp.float32
        )
    for layer in range(layers):
        bias_grad[layer : layer + 1, :] = jnp.sum(
            db[layer].astype(jnp.float32), axis=0, keepdims=True
        )
    for copy in copies:
        copy.wait()


def write_outputs(xa, db, counts, ga, crossed, pgrad):
    layers, _, in_width = xa.shape
    out_width = db.shape[2]
    feats, shard_rows, _ = counts.shape
    entry = in_width // feats
    tiles = in_width // math.gcd(in_width, 256)
    f32 = jnp.float32
    vmem = pl.BlockSpec(memory_space=pltpu.VMEM)
    return pl.pallas_call(
        output_kernel,
        out_shape=(
            jax.ShapeDtypeStruct((layers, in_width, out_width), f32),
            jax.ShapeDtypeStruct((layers, out_width), f32),
            jax.ShapeDtypeStruct((feats, shard_rows, entry), f32),
            jax.ShapeDtypeStruct(crossed.shape, crossed.dtype),
            jax.ShapeDtypeStruct(pgrad.shape, f32),
        ),
        in_specs=[pl.BlockSpec(memory_space=pl.ANY)] * 6,
        out_specs=(pl.BlockSpec(memory_space=pl.ANY), vmem, vmem, vmem, vmem),
        scratch_shapes=[
            pltpu.VMEM(xa.shape, xa.dtype),
            pltpu.VMEM(db.shape, db.dtype),
            pltpu.VMEM(counts.shape, counts.dtype),
            pltpu.VMEM(ga.shape, ga.dtype),
            pltpu.VMEM((layers, in_width, out_width), f32),
            pltpu.SemaphoreType.DMA((2 * layers + 4,)),
            pltpu.SemaphoreType.DMA((layers * tiles,)),
        ],
        compiler_params=pltpu.CompilerParams(vmem_limit_bytes=56 * 1024 * 1024),
    )(xa, db, counts, ga, crossed, pgrad)


def body(tables, bag_index, cross_weight, cross_bias, upstream):
    feat_count, shard_rows, entry_width = tables.shape
    batch_rows = bag_index.shape[0]
    layers, in_width, out_width = cross_weight.shape
    block_rows = upstream.shape[0]
    sizes = tuple(lax.axis_size(axis) for axis in ("section", "row", "col"))
    np_count = sizes[0] * sizes[1]
    col_count = sizes[2]
    ratio = in_width // out_width
    ids = jnp.transpose(bag_index, (1, 2, 0))
    bf16, f32 = jnp.bfloat16, jnp.float32
    vmem = pl.BlockSpec(memory_space=pltpu.VMEM)
    hbm = pl.BlockSpec(memory_space=pl.ANY)
    dma = pltpu.SemaphoreType.DMA
    counts, xa, db, crossed, pooled_grad, full_grad = pl.pallas_call(
        functools.partial(kernel, sizes),
        out_shape=(
            jax.ShapeDtypeStruct((feat_count, shard_rows, batch_rows), bf16),
            jax.ShapeDtypeStruct((layers, batch_rows, in_width), bf16),
            jax.ShapeDtypeStruct((layers, batch_rows, out_width), bf16),
            jax.ShapeDtypeStruct((block_rows, in_width), bf16),
            jax.ShapeDtypeStruct((block_rows, in_width), f32),
            jax.ShapeDtypeStruct((batch_rows, in_width), bf16),
        ),
        in_specs=[vmem, vmem, vmem, vmem, pl.BlockSpec(memory_space=pl.ANY)],
        out_specs=(hbm, hbm, hbm, vmem, vmem, hbm),
        scratch_shapes=[
            pltpu.VMEM((layers, in_width, out_width), bf16),
            pltpu.VMEM((feat_count, shard_rows, batch_rows), bf16),
            pltpu.VMEM((batch_rows, in_width), bf16),
            pltpu.VMEM((np_count, block_rows, in_width), bf16),
            pltpu.VMEM((layers + 1, sizes[1], block_rows, in_width), bf16),
            pltpu.VMEM((layers, batch_rows, in_width), bf16),
            pltpu.VMEM((layers, batch_rows, out_width), bf16),
            pltpu.VMEM((batch_rows, in_width), bf16),
            pltpu.VMEM((layers, block_rows, in_width), bf16),
            pltpu.VMEM((layers, batch_rows, out_width), bf16),
            pltpu.VMEM((layers, ratio * col_count, block_rows, out_width), bf16),
            pltpu.VMEM((layers, batch_rows, in_width), bf16),
            pltpu.VMEM((layers, np_count, block_rows, in_width), bf16),
            pltpu.VMEM((layers, block_rows, in_width), f32),
            dma((layers,)),
            dma((2 * layers + 2,)),
            dma((np_count,)),
            dma((np_count,)),
            dma((layers + 1, np_count)),
            dma((layers + 1, np_count)),
            dma((layers, ratio * col_count)),
            dma((layers, np_count)),
            dma((layers, np_count)),
            dma((layers, ratio * col_count)),
            dma((layers, np_count)),
            dma((layers, np_count)),
        ],
        compiler_params=pltpu.CompilerParams(
            collective_id=0, has_side_effects=True, vmem_limit_bytes=56 * 1024 * 1024
        ),
    )(ids, tables, upstream, cross_bias, cross_weight)
    weight_grad, bias_grad, table_grad, crossed, pooled_grad = write_outputs(
        xa, db, counts, full_grad, crossed, pooled_grad
    )
    return crossed, pooled_grad, table_grad, weight_grad, bias_grad


def solution(mesh):
    return jax.shard_map(
        body,
        mesh=mesh,
        in_specs=(
            P("col", ("section", "row"), None),
            P(None, "col", None),
            P(None, "col", ("section", "row")),
            P(),
            P(("section", "row"), "col"),
        ),
        out_specs=(
            P(("section", "row"), "col"),
            P(("section", "row"), "col"),
            P("col", ("section", "row"), None),
            P(None, "col", ("section", "row")),
            P(None, ("section", "row")),
        ),
        check_vma=False,
    )
```
